128 devices in a mesh: wave: 64 (over y, x, z), point: 2 (over core).
Axes of the slice: x: 4, y: 4, z: 4, core: 2. Of those that a mesh axis runs over, the one named last changes fastest.
Arguments:
- cube: float32 [2, 4096, 32768], P('point', 'wave'), may hold values from 0 to 3
- psf: bfloat16 [2, 64, 1024, 1024], P('point', 'wave'), may hold values from -0.09375 to 0.09375
- spectra: float32 [200, 4096], P(None, 'wave'), may hold values from 0 to 1
- morph: float32 [200, 1024], P(None, 'wave'), may hold values from 0 to 1
- src_tile: int32 [2, 200], P('point'), may hold values from 0 to 32
- wave_range: int32 [200, 2], replicated, may hold values from 0 to 4096, as said below
- spec_step: float32 [200], replicated, may hold values from 0.00048828125 to 0.00390625
- morph_step: float32 [200], replicated, may hold values from 0.00012207031 to 0.0009765625
Outputs:
- new_spectra: float32 [200, 4096], P(None, 'wave')
- new_morph: float32 [200, 1024], P(None, 'wave')
The draws below stay inside these ranges and needn't reach their ends.
Inputs may be any that keep to these rules, and one draw needn't show every extreme that they name: wave_range[s, 0] < wave_range[s, 1]. `src_tile`: the value 32 marks a source absent from that pointing.
All inputs are finite; a program needn't handle non-finite values.
Results may differ from the reference program's by a relative error of at most 0.0039.
Values may be sent and summed in bfloat16 or wider, within the bound.
No kernel may reach another device: no remote copies, remote signals or barrier semaphores. Data moves between devices by JAX's collectives and lax.ppermute only.
A program may use at most 192 MiB of HBM per device.

```python
import math
import jax
import jax.numpy as jnp
from jax import lax

LAM_DEV = 64
TILE_PIX = 1024
TILES = 32
SOURCES = 200
LAM = 4096
PIXELS = 32768
POINTS = 2
PSF_BLOCKS = 64


def draw_wave_range(key, part):
    first_key, second_key = jax.random.split(jax.random.fold_in(key, 11))
    start = jax.random.randint(first_key, (SOURCES,), 0, LAM // 2)
    width = jax.random.randint(second_key, (SOURCES,), LAM // 8 + 1, LAM // 2 + 1)
    stop = start + width
    start = start.at[0].set(0)
    stop = stop.at[0].set(LAM)
    return jnp.stack([start, stop], axis=1).astype(jnp.int32)


def place_ends(drawn, rng, low, top_value):
    place = [jax.random.randint(jax.random.fold_in(rng, axis), (), 0, length) for axis, length in enumerate(drawn.shape)]
    longest = drawn.shape.index(max(drawn.shape))
    next_to = place[:longest] + [(place[longest] + 1) % drawn.shape[longest]] + place[longest + 1:]
    return drawn.at[tuple(place)].set(low).at[tuple(next_to)].set(top_value)


def block_levels(rng, shape, cuts, least, high):
    loudness = 1.0
    for axis_at, blocks in cuts:
        heights = jax.random.uniform(jax.random.fold_in(jax.random.fold_in(rng, 6), axis_at), (blocks,), jnp.float32, least / len(cuts), high / len(cuts))
        loudness = loudness * jnp.repeat(jnp.exp(heights), shape[axis_at] // blocks).reshape((-1,) + (1,) * (len(shape) - 1 - axis_at))
    return loudness


def normal_values(key, dims, scale, bound, cuts=(), held_as=jnp.bfloat16):
    drawn = jax.random.normal(key, dims, jnp.float32) * scale
    if len(cuts) > 0:
        drawn = block_levels(key, dims, cuts, -0.22, 0.18) * drawn
    return jnp.clip(drawn, min=-bound, max=bound).astype(held_as)


def setup_inputs(seed: int = 0) -> dict:
    splits = jax.random.split(jax.random.key(seed), 9)
    cube = jnp.clip(3.0 * jax.random.uniform(splits[0], (POINTS, LAM, PIXELS), jnp.float32) ** block_levels(splits[0], (POINTS, LAM, PIXELS), ((0, 2), (1, 64)), -0.2, 0.2), 0.0, 3.0)
    psf = normal_values(splits[1], (POINTS, PSF_BLOCKS, TILE_PIX, TILE_PIX), (4 * TILE_PIX) ** -0.5, 0.09375, ((0, 2), (1, 64)))
    spectra = jnp.clip(1.0 * jax.random.uniform(splits[2], (SOURCES, LAM), jnp.float32) ** block_levels(splits[2], (SOURCES, LAM), ((1, 64),), -0.2, 0.2), 0.0, 1.0)
    morph = jnp.clip(1.0 * jax.random.uniform(splits[3], (SOURCES, TILE_PIX), jnp.float32) ** block_levels(splits[3], (SOURCES, TILE_PIX), ((1, 64),), -0.2, 0.2), 0.0, 1.0)
    src_tile = place_ends(jax.random.randint(splits[4], (POINTS, SOURCES), 0, TILES + 1), jax.random.fold_in(splits[4], 1), 0, TILES).astype(jnp.int32)
    wave_range = draw_wave_range(jax.random.fold_in(splits[8], 71), 0)
    spec_step = jnp.clip(jnp.exp(jax.random.uniform(splits[6], (SOURCES,), jnp.float32, math.log(0.00048828125), math.log(0.00390625))), 0.00048828125, 0.00390625)
    morph_step = jnp.clip(jnp.exp(jax.random.uniform(splits[7], (SOURCES,), jnp.float32, math.log(0.00012207031), math.log(0.0009765625))), 0.00012207031, 0.0009765625)
    return dict(cube=cube, psf=psf, spectra=spectra, morph=morph, src_tile=src_tile, wave_range=wave_range, spec_step=spec_step, morph_step=morph_step)


def slab_terms(cube_blk, psf_blk, spec_blk, morph_b, onehot):
    blurred = (morph_b.astype(jnp.float32) + jnp.dot(morph_b, psf_blk, preferred_element_type=jnp.float32)).astype(jnp.bfloat16)
    placed = (blurred[:, :, None] * onehot[:, None, :]).reshape(SOURCES, PIXELS)
    spec_b = spec_blk.astype(jnp.bfloat16)
    model = jnp.dot(spec_b.T, placed, preferred_element_type=jnp.float32)
    resid = cube_blk - model
    resid_b = resid.astype(jnp.bfloat16)
    corr_spec = jnp.einsum("sx,lx->sl", placed.astype(jnp.float32), resid_b.astype(jnp.float32))
    back = jnp.einsum("lrt,qr->lqt", resid_b.reshape(LAM_DEV, TILE_PIX, TILES).astype(jnp.float32), psf_blk.astype(jnp.float32))
    adjoint = (resid + back.reshape(LAM_DEV, PIXELS)).astype(jnp.bfloat16)
    weighted = jnp.dot(spec_b, adjoint, preferred_element_type=jnp.float32).reshape(SOURCES, TILE_PIX, TILES)
    corr_morph = jnp.sum(weighted * onehot[:, None, :].astype(jnp.float32), axis=2)
    return corr_spec, corr_morph


def reference(cube, psf, spectra, morph, src_tile, wave_range, spec_step, morph_step):
    morph_b = morph.astype(jnp.bfloat16)
    spec_blocks = spectra.reshape(SOURCES, PSF_BLOCKS, LAM_DEV).transpose(1, 0, 2)
    corr_spec = jnp.zeros((SOURCES, LAM), jnp.float32)
    corr_morph = jnp.zeros((SOURCES, TILE_PIX), jnp.float32)
    for point in range(POINTS):
        onehot = (src_tile[point][:, None] == jnp.arange(TILES, dtype=jnp.int32)[None, :]).astype(jnp.bfloat16)

        def step_block(carry, inputs):
            cube_blk, psf_blk, spec_blk = inputs
            part_spec, part_morph = slab_terms(cube_blk, psf_blk, spec_blk, morph_b, onehot)
            return carry + part_morph, part_spec

        total_morph, spec_parts = lax.scan(step_block, jnp.zeros((SOURCES, TILE_PIX), jnp.float32),
                                           (cube[point].reshape(PSF_BLOCKS, LAM_DEV, PIXELS), psf[point], spec_blocks))
        corr_morph = corr_morph + total_morph
        corr_spec = corr_spec + spec_parts.transpose(1, 0, 2).reshape(SOURCES, LAM)
    lam_index = jnp.arange(LAM, dtype=jnp.int32)
    inside = (lam_index[None, :] >= wave_range[:, 0:1]) & (lam_index[None, :] < wave_range[:, 1:2])
    new_spectra = jnp.where(inside, jnp.maximum(spectra + spec_step[:, None] * corr_spec, 0.0), 0.0)
    new_morph = jnp.maximum(morph + morph_step[:, None] * corr_morph, 0.0)
    return new_spectra, new_morph
```

```python
import jax
import jax.numpy as jnp
from jax import lax
from jax.experimental import pallas as pl
from jax.experimental.pallas import tpu as pltpu
from jax.sharding import PartitionSpec as P

BF = jnp.bfloat16
F32 = jnp.float32
S = 256
L8 = 8
TILES = 32
Q = 1024
QI = 4
J = 256


def dot(a, b):
    return jnp.dot(a, b, preferred_element_type=F32)


def dot_t(a, b):
    return lax.dot_general(a, b, (((0,), (0,)), ((), ())), preferred_element_type=F32)


def split(x):
    hi = x.astype(BF)
    return hi, (x - hi.astype(F32)).astype(BF)


def present(tile):
    return lax.broadcasted_iota(jnp.int32, (TILES, S), 0) == tile


def same_tile(tile):
    onehot = jnp.where(present(tile), 1.0, 0.0).astype(BF)
    return dot_t(onehot, onehot)


def prep_kernel(tile_ref, spec_ref, x_ref, rhi_ref, rlo_ref, g_ref, mhi_ref, mlo_ref, at_ref, acc_ref):
    step = pl.program_id(0)
    here = present(tile_ref[...])
    spec8 = spec_ref[pl.ds(pl.multiple_of(step * L8, L8), L8), :].astype(BF).astype(F32)
    for l in range(L8):
        at_ref[l * TILES : (l + 1) * TILES, :] = jnp.where(here, spec8[l : l + 1, :], 0.0).astype(BF)
    lane = lax.broadcasted_iota(jnp.int32, (64, 128), 1)
    low = lane < 64
    even = (lane % 64) < 32
    for h in range(2):
        for c in range(4):
            p = [x_ref[0, pl.ds(c * 512 + 4 * h + g, 64, stride=8), :] for g in range(4)]
            u = [None] * 4
            for a in range(2):
                u[a] = jnp.where(low, p[a], pltpu.roll(p[a + 2], 64, 1))
                u[a + 2] = jnp.where(low, pltpu.roll(p[a], 64, 1), p[a + 2])
            for a in (0, 2):
                r = (
                    jnp.where(even, u[a], pltpu.roll(u[a + 1], 32, 1)),
                    jnp.where(even, pltpu.roll(u[a], 96, 1), u[a + 1]),
                )
                for b in range(2):
                    hi, lo = split(r[b])
                    rows = slice((a + b) * J + c * 64, (a + b) * J + (c + 1) * 64)
                    cols = slice(h * 128, (h + 1) * 128)
                    rhi_ref[rows, cols] = hi
                    rlo_ref[rows, cols] = lo
    part = dot(rhi_ref[...], at_ref[...]) + dot(rlo_ref[...], at_ref[...])

    @pl.when(step == 0)
    def _():
        acc_ref[...] = part

    @pl.when(step > 0)
    def _():
        acc_ref[...] += part

    @pl.when(step == pl.num_programs(0) - 1)
    def _():
        for qi in range(QI):
            for k in range(2):
                g_ref[k, pl.ds(qi, J, stride=QI), :] = acc_ref[qi * J : (qi + 1) * J, k * 128 : (k + 1) * 128]
        spec_b = spec_ref[...].astype(BF)
        gram = dot_t(spec_b, spec_b) * same_tile(tile_ref[...])
        hi, lo = split(gram)
        mhi_ref[...] = hi
        mlo_ref[...] = lo


def prep(tile, spec, cube):
    steps = spec.shape[0] // L8
    whole = lambda i: (0, 0)
    return pl.pallas_call(
        prep_kernel,
        grid=(steps,),
        in_specs=[
            pl.BlockSpec((1, S), whole),
            pl.BlockSpec(spec.shape, whole),
            pl.BlockSpec((1, 2048, 128), lambda i: (i, 0, 0)),
        ],
        out_specs=[
            pl.BlockSpec((Q, 256), lambda i: (0, i)),
            pl.BlockSpec((Q, 256), lambda i: (0, i)),
            pl.BlockSpec((2, Q, 128), lambda i: (0, 0, 0)),
            pl.BlockSpec((S, S), whole),
            pl.BlockSpec((S, S), whole),
        ],
        out_shape=[
            jax.ShapeDtypeStruct((Q, 256 * steps), BF),
            jax.ShapeDtypeStruct((Q, 256 * steps), BF),
            jax.ShapeDtypeStruct((2, Q, 128), F32),
            jax.ShapeDtypeStruct((S, S), BF),
            jax.ShapeDtypeStruct((S, S), BF),
        ],
        scratch_shapes=[pltpu.VMEM((256, S), BF), pltpu.VMEM((Q, S), F32)],
        compiler_params=pltpu.CompilerParams(vmem_limit_bytes=32 << 20),
        cost_estimate=pl.CostEstimate(flops=4 * Q * 2048 * S, transcendentals=0, bytes_accessed=17 << 20),
        name="prep",
    )(tile, spec, cube)


def morph_kernel(m_ref, psf_ref, g_ref, mhi_ref, mlo_ref, corr_ref, b_ref):
    morph_b = m_ref[...].T
    blurred = (morph_b.astype(F32) + dot(morph_b, psf_ref[...])).astype(BF)
    blurred_t = blurred.T
    for k in range(2):
        b_ref[k] = blurred_t[:, k * 128 : (k + 1) * 128].astype(F32)
    model = dot(blurred_t, mhi_ref[...]) + dot(blurred_t, mlo_ref[...])
    w = jnp.concatenate([g_ref[0], g_ref[1]], axis=1) - model
    hi, lo = split(w)
    corr_ref[...] = w + dot(psf_ref[...], hi) + dot(psf_ref[...], lo)


def morph_part(morph_all, psf, g, mhi, mlo):
    return pl.pallas_call(
        morph_kernel,
        out_shape=[jax.ShapeDtypeStruct((Q, S), F32), jax.ShapeDtypeStruct((2, Q, 128), F32)],
        compiler_params=pltpu.CompilerParams(vmem_limit_bytes=32 << 20),
        cost_estimate=pl.CostEstimate(flops=6 * Q * Q * S, transcendentals=0, bytes_accessed=5 << 20),
        name="morph_part",
    )(morph_all, psf, g, mhi, mlo)


def spec_kernel(tile_ref, spec_ref, b_ref, rhi_ref, rlo_ref, c_ref, bp_ref):
    step = pl.program_id(0)

    @pl.when(step == 0)
    def _():
        for qi in range(QI):
            for k in range(2):
                rows = b_ref[k, pl.ds(qi, J, stride=QI), :]
                bp_ref[k * 128 : (k + 1) * 128, qi * J : (qi + 1) * J] = rows.T.astype(BF)
        bp = bp_ref[...]
        gram = lax.dot_general(bp, bp, (((1,), (1,)), ((), ())), preferred_element_type=F32)
        hi, lo = split(gram * same_tile(tile_ref[...]))
        spec_b = spec_ref[...].astype(BF)
        c_ref[...] = -(dot(spec_b, hi) + dot(spec_b, lo))

    bp = bp_ref[...]
    y = dot(bp, rhi_ref[...]) + dot(bp, rlo_ref[...])
    y_t = y.T.reshape(L8, TILES, S)
    rows = jnp.sum(jnp.where(present(tile_ref[...])[None], y_t, 0.0), axis=1)
    at = pl.ds(pl.multiple_of(step * L8, L8), L8)
    c_ref[at, :] += rows


def spec_part(tile, spec, b, rhi, rlo):
    steps = spec.shape[0] // L8
    whole = lambda i: (0, 0)
    return pl.pallas_call(
        spec_kernel,
        grid=(steps,),
        in_specs=[
            pl.BlockSpec((1, S), whole),
            pl.BlockSpec(spec.shape, whole),
            pl.BlockSpec((2, Q, 128), lambda i: (0, 0, 0)),
            pl.BlockSpec((Q, 256), lambda i: (0, i)),
            pl.BlockSpec((Q, 256), lambda i: (0, i)),
        ],
        out_specs=pl.BlockSpec(spec.shape, whole),
        out_shape=jax.ShapeDtypeStruct(spec.shape, F32),
        scratch_shapes=[pltpu.VMEM((S, Q), BF)],
        compiler_params=pltpu.CompilerParams(vmem_limit_bytes=32 << 20),
        cost_estimate=pl.CostEstimate(flops=4 * Q * 2048 * S, transcendentals=0, bytes_accessed=9 << 20),
        name="spec_part",
    )(tile, spec, b, rhi, rlo)


SWAP = [(0, 1), (1, 0)]


def on_device(cube, psf, spectra, morph, src_tile, wave_range, spec_step, morph_step):
    sources, depth = spectra.shape
    own = morph.shape[1]
    waves = Q // own
    pad = S - sources
    morph_t = morph.T
    mine = jnp.pad(morph_t.astype(BF), ((0, 0), (0, pad)))
    morph_all = lax.all_to_all(
        jnp.broadcast_to(mine[None], (waves, own, S)), "wave", split_axis=0, concat_axis=0, tiled=True
    ).reshape(Q, S)
    spec_t = spectra.T
    spec = jnp.pad(spec_t, ((0, 0), (0, pad)))
    tile = jnp.pad(src_tile, ((0, 0), (0, pad)), constant_values=TILES)
    groups = depth // L8
    rows = cube.reshape(groups, L8, J, 128).transpose(0, 2, 1, 3).reshape(groups, J * L8, 128)
    rhi, rlo, g, mhi, mlo = prep(tile, spec, rows)
    corr, blurred = morph_part(morph_all, psf[0, 0], g, mhi, mlo)
    parts = lax.all_to_all(corr.reshape(waves, own, S), "wave", split_axis=0, concat_axis=0, tiled=True)
    corr_spec = spec_part(tile, spec, blurred, rhi, rlo)
    corr_spec = (corr_spec + lax.ppermute(corr_spec, "point", SWAP))[:, :sources]
    lam = lax.axis_index("wave") * depth + jnp.arange(depth, dtype=jnp.int32)
    inside = (lam[:, None] >= wave_range[None, :, 0]) & (lam[:, None] < wave_range[None, :, 1])
    new_spectra = jnp.where(inside, jnp.maximum(spec_t + spec_step[None, :] * corr_spec, 0.0), 0.0)
    corr_morph = jnp.sum(parts, axis=0)
    corr_morph = (corr_morph + lax.ppermute(corr_morph, "point", SWAP))[:, :sources]
    new_morph = jnp.maximum(morph_t + morph_step[None, :] * corr_morph, 0.0)
    return (new_spectra.T, new_morph.T)


def solution(mesh):
    return jax.shard_map(
        on_device,
        mesh=mesh,
        in_specs=(
            P("point", "wave", None),
            P("point", "wave", None, None),
            P(None, "wave"),
            P(None, "wave"),
            P("point", None),
            P(),
            P(),
            P(),
        ),
        out_specs=(P(None, "wave"), P(None, "wave")),
        check_vma=False,
    )
```

```python
import jax
import jax.numpy as jnp
from jax import lax
from jax.experimental import pallas as pl
from jax.experimental.pallas import tpu as pltpu
from jax.sharding import PartitionSpec as P

BF = jnp.bfloat16
F32 = jnp.float32
S = 256
L8 = 8
TILES = 32
Q = 1024
QI = 4
J = 256


def dot(a, b):
    return jnp.dot(a, b, preferred_element_type=F32)


def dot_t(a, b):
    return lax.dot_general(a, b, (((0,), (0,)), ((), ())), preferred_element_type=F32)


def split(x):
    hi = x.astype(BF)
    return hi, (x - hi.astype(F32)).astype(BF)


def present(tile):
    return lax.broadcasted_iota(jnp.int32, (TILES, S), 0) == tile


def same_tile(tile):
    onehot = jnp.where(present(tile), 1.0, 0.0).astype(BF)
    return dot_t(onehot, onehot)


def spread_kernel(morph_ref, out_ref):
    mine = jnp.concatenate([morph_ref[...], jnp.zeros((morph_ref.shape[0], S - morph_ref.shape[1]), F32)], axis=1)
    out_ref[...] = jnp.broadcast_to(mine.astype(BF)[None], out_ref.shape)


def spread(morph_t, copies):
    return pl.pallas_call(
        spread_kernel,
        out_shape=jax.ShapeDtypeStruct((copies, morph_t.shape[0], S), BF),
        name="spread",
    )(morph_t)


def widen(ref, value):
    rest = jnp.full((ref.shape[0], S - ref.shape[1]), value, ref.dtype)
    return jnp.concatenate([ref[...], rest], axis=1)


def place(k):
    return (k % 2) * 2 + k // 2


def prep_kernel(
    tile_hbm, spec_hbm, x_hbm, r_hbm, g_ref, mhi_ref, mlo_ref, at_ref, x_ref, r_ref, tile_ref, spec_ref, sem, out_sem, small_sem
):
    steps = x_hbm.shape[0]
    small = [
        pltpu.make_async_copy(tile_hbm, tile_ref, small_sem.at[0]),
        pltpu.make_async_copy(spec_hbm, spec_ref, small_sem.at[1]),
    ]
    for copy in small:
        copy.start()
    for i in range(steps):
        pltpu.make_async_copy(x_hbm.at[i], x_ref.at[i], sem.at[i]).start()
    for copy in small:
        copy.wait()
    tile = widen(tile_ref, TILES)
    here = present(tile)
    spec = widen(spec_ref, 0.0)
    spec_b = spec.astype(BF)
    spec_f = spec_b.astype(F32)
    for l in range(L8 * steps):
        block = jnp.where(here, spec_f[l : l + 1, :], 0.0).astype(BF)
        turned = (l // 4) * 4 + (l + 1) % 4
        at_ref[0, l * TILES : (l + 1) * TILES, :] = block
        at_ref[1, turned * TILES : (turned + 1) * TILES, :] = block
    hi, lo = split(dot_t(spec_b, spec_b) * same_tile(tile))
    mhi_ref[...] = hi
    mlo_ref[...] = lo
    lane = lax.broadcasted_iota(jnp.int32, (CHUNK, 128), 1)
    low = lane < 64
    even = (lane % 64) < 32
    acc = [None] * QI
    for i in range(steps):
        pltpu.make_async_copy(x_hbm.at[i], x_ref.at[i], sem.at[i]).wait()
        for h in range(2):
            for c in range(J // CHUNK):
                p = [x_ref[i, pl.ds(c * 8 * CHUNK + 4 * h + g, CHUNK, stride=8), :] for g in range(4)]
                u = [None] * 4
                for a in range(2):
                    turn = pltpu.roll(jnp.where(low, p[a + 2], p[a]), 64, 1)
                    u[a] = jnp.where(low, p[a], turn)
                    u[a + 2] = jnp.where(low, turn, p[a + 2])
                for a in range(2):
                    turn = pltpu.roll(u[2 * a + 1], 32, 1)
                    pair = (jnp.where(even, u[2 * a], turn), jnp.where(even, turn, u[2 * a]))
                    for b in range(2):
                        hi, lo = split(pair[b])
                        first = place(2 * a + b) * J + c * CHUNK
                        r_ref[i, 0, first : first + CHUNK, h * 128 : (h + 1) * 128] = hi
                        r_ref[i, 1, first : first + CHUNK, h * 128 : (h + 1) * 128] = lo
        for k in range(QI):
            at = at_ref[k % 2, i * 256 : (i + 1) * 256, :]
            rows = slice(place(k) * J, (place(k) + 1) * J)
            part = dot(r_ref[i, 0, rows, :], at) + dot(r_ref[i, 1, rows, :], at)
            acc[k] = part if i == 0 else acc[k] + part
        pltpu.make_async_copy(r_ref.at[i], r_hbm.at[i], out_sem.at[i]).start()
    for k in range(QI):
        for n in range(2):
            g_ref[n, pl.ds(k, J, stride=QI), :] = acc[k][:, n * 128 : (n + 1) * 128]
    for i in range(steps):
        pltpu.make_async_copy(r_ref.at[i], r_hbm.at[i], out_sem.at[i]).wait()


IN_VMEM = pl.BlockSpec(memory_space=pltpu.VMEM)
IN_HBM = pl.BlockSpec(memory_space=pltpu.HBM)
CHUNK = 32


def in_hbm(x):
    return pltpu.with_memory_space_constraint(x, pltpu.HBM)


def prep(tile, spec, cube):
    steps = cube.shape[0]
    return pl.pallas_call(
        prep_kernel,
        in_specs=[IN_HBM] * 3,
        out_specs=[IN_HBM] + [IN_VMEM] * 3,
        out_shape=[
            pltpu.HBM((steps, 2, Q, 256), BF),
            jax.ShapeDtypeStruct((2, Q, 128), F32),
            jax.ShapeDtypeStruct((S, S), BF),
            jax.ShapeDtypeStruct((S, S), BF),
        ],
        scratch_shapes=[
            pltpu.VMEM((2, 256 * steps, S), BF),
            pltpu.VMEM((steps, 2048, 128), F32),
            pltpu.VMEM((steps, 2, Q, 256), BF),
            pltpu.VMEM(tile.shape, jnp.int32),
            pltpu.VMEM(spec.shape, F32),
            pltpu.SemaphoreType.DMA((steps,)),
            pltpu.SemaphoreType.DMA((steps,)),
            pltpu.SemaphoreType.DMA((2,)),
        ],
        compiler_params=pltpu.CompilerParams(vmem_limit_bytes=28 << 20),
        cost_estimate=pl.CostEstimate(flops=4 * Q * 2048 * S, transcendentals=0, bytes_accessed=17 << 20),
        name="prep",
    )(in_hbm(tile), in_hbm(spec), in_hbm(cube))


def morph_kernel(m_ref, psf_hbm, g_ref, mhi_ref, mlo_ref, corr_ref, b_ref, psf_ref, sem):
    parts = Q // J
    for i in range(parts):
        pltpu.make_async_copy(psf_hbm.at[pl.ds(i * J, J)], psf_ref.at[pl.ds(i * J, J)], sem.at[i]).start()
    morph_b = m_ref[...].T
    blurred = morph_b.astype(F32)
    for i in range(parts):
        pltpu.make_async_copy(psf_hbm.at[pl.ds(i * J, J)], psf_ref.at[pl.ds(i * J, J)], sem.at[i]).wait()
        blurred = blurred + dot(morph_b[:, i * J : (i + 1) * J], psf_ref[i * J : (i + 1) * J, :])
    blurred = blurred.astype(BF)
    blurred_t = blurred.T
    for k in range(2):
        b_ref[k] = blurred_t[:, k * 128 : (k + 1) * 128].astype(F32)
    model = dot(blurred_t, mhi_ref[...]) + dot(blurred_t, mlo_ref[...])
    w = jnp.concatenate([g_ref[0], g_ref[1]], axis=1) - model
    hi, lo = split(w)
    corr_ref[...] = (w + dot(psf_ref[...], hi) + dot(psf_ref[...], lo)).astype(corr_ref.dtype)


def morph_part(morph_all, psf, g, mhi, mlo):
    return pl.pallas_call(
        morph_kernel,
        in_specs=[IN_VMEM, IN_HBM, IN_VMEM, IN_VMEM, IN_VMEM],
        out_shape=[jax.ShapeDtypeStruct((Q, S), BF), jax.ShapeDtypeStruct((2, Q, 128), F32)],
        scratch_shapes=[pltpu.VMEM(psf.shape, BF), pltpu.SemaphoreType.DMA((Q // J,))],
        compiler_params=pltpu.CompilerParams(vmem_limit_bytes=12 << 20),
        cost_estimate=pl.CostEstimate(flops=6 * Q * Q * S, transcendentals=0, bytes_accessed=5 << 20),
        name="morph_part",
    )(morph_all, in_hbm(psf), g, mhi, mlo)


def spec_kernel(tile_ref, spec_ref, b_ref, r_hbm, c_ref, bp_ref, r_ref, sem):
    steps = r_hbm.shape[0]
    for i in range(steps):
        pltpu.make_async_copy(r_hbm.at[i], r_ref.at[i], sem.at[i]).start()
    tile = widen(tile_ref, TILES)
    here = present(tile)[None]
    for k in range(QI):
        for n in range(2):
            rows = b_ref[n, pl.ds(k, J, stride=QI), :]
            bp_ref[n * 128 : (n + 1) * 128, place(k) * J : (place(k) + 1) * J] = rows.T.astype(BF)
    bp = bp_ref[...]
    gram = lax.dot_general(bp, bp, (((1,), (1,)), ((), ())), preferred_element_type=F32)
    hi, lo = split(gram * same_tile(tile))
    spec_b = widen(spec_ref, 0.0).astype(BF)
    model = dot(spec_b, hi) + dot(spec_b, lo)
    for i in range(steps):
        pltpu.make_async_copy(r_hbm.at[i], r_ref.at[i], sem.at[i]).wait()
        y = [None] * 2
        for e in range(2):
            rows = slice(e * 2 * J, (e + 1) * 2 * J)
            y[e] = dot(bp[:, rows], r_ref[i, 0, rows, :]) + dot(bp[:, rows], r_ref[i, 1, rows, :])
        for h in range(2):
            cols = slice(h * 128, (h + 1) * 128)
            y_t = (y[0][:, cols] + pltpu.roll(y[1][:, cols], 96, 1)).T.reshape(4, TILES, S)
            first = i * L8 + 4 * h
            c_ref[first : first + 4, :] = jnp.sum(jnp.where(here, y_t, 0.0), axis=1) - model[first : first + 4, :]


def spec_part(tile, spec, b, r):
    return pl.pallas_call(
        spec_kernel,
        in_specs=[IN_VMEM] * 3 + [IN_HBM],
        out_specs=IN_VMEM,
        out_shape=jax.ShapeDtypeStruct((spec.shape[0], S), F32),
        scratch_shapes=[pltpu.VMEM((S, Q), BF), pltpu.VMEM(r.shape, BF), pltpu.SemaphoreType.DMA(r.shape[:1])],
        compiler_params=pltpu.CompilerParams(vmem_limit_bytes=16 << 20),
        cost_estimate=pl.CostEstimate(flops=4 * Q * 2048 * S, transcendentals=0, bytes_accessed=9 << 20),
        name="spec_part",
    )(tile, spec, b, in_hbm(r))


SWAP = [(0, 1), (1, 0)]


def on_device(cube, psf, spectra, morph, src_tile, wave_range, spec_step, morph_step):
    sources, depth = spectra.shape
    own = morph.shape[1]
    waves = Q // own
    morph_t = morph.T
    spec_t = spectra.T
    morph_all = lax.all_to_all(spread(morph_t, waves), "wave", split_axis=0, concat_axis=0, tiled=True).reshape(Q, S)
    groups = depth // L8
    rows = cube.reshape(groups, L8, J, 128).transpose(0, 2, 1, 3).reshape(groups, J * L8, 128)
    r, g, mhi, mlo = prep(src_tile, spec_t, rows)
    corr, blurred = morph_part(morph_all, psf[0, 0], g, mhi, mlo)
    parts = lax.all_to_all(corr.reshape(waves, own, S), "wave", split_axis=0, concat_axis=0, tiled=True)
    corr_spec = spec_part(src_tile, spec_t, blurred, r)
    corr_spec = (corr_spec + lax.ppermute(corr_spec, "point", SWAP))[:, :sources]
    lam = lax.axis_index("wave") * depth + jnp.arange(depth, dtype=jnp.int32)
    inside = (lam[:, None] >= wave_range[None, :, 0]) & (lam[:, None] < wave_range[None, :, 1])
    new_spectra = jnp.where(inside, jnp.maximum(spec_t + spec_step[None, :] * corr_spec, 0.0), 0.0)
    corr_morph = jnp.sum(parts.astype(F32), axis=0)
    corr_morph = (corr_morph + lax.ppermute(corr_morph, "point", SWAP))[:, :sources]
    new_morph = jnp.maximum(morph_t + morph_step[None, :] * corr_morph, 0.0)
    return (new_spectra.T, new_morph.T)


def solution(mesh):
    return jax.shard_map(
        on_device,
        mesh=mesh,
        in_specs=(
            P("point", "wave", None),
            P("point", "wave", None, None),
            P(None, "wave"),
            P(None, "wave"),
            P("point", None),
            P(),
            P(),
            P(),
        ),
        out_specs=(P(None, "wave"), P(None, "wave")),
        check_vma=False,
    )
```

```python
import jax
import jax.numpy as jnp
from jax import lax
from jax.experimental import pallas as pl
from jax.experimental.pallas import tpu as pltpu
from jax.sharding import PartitionSpec as P

BF = jnp.bfloat16
F32 = jnp.float32
S = 256
L8 = 8
TILES = 32
Q = 1024
QI = 4
J = 256


def dot(a, b):
    return jnp.dot(a, b, preferred_element_type=F32)


def dot_t(a, b):
    return lax.dot_general(a, b, (((0,), (0,)), ((), ())), preferred_element_type=F32)


def split(x):
    hi = x.astype(BF)
    return hi, (x - hi.astype(F32)).astype(BF)


def present(tile):
    return lax.broadcasted_iota(jnp.int32, (TILES, S), 0) == tile


def same_tile(tile):
    onehot = jnp.where(present(tile), 1.0, 0.0).astype(BF)
    return dot_t(onehot, onehot)


def widen(ref, value):
    rest = jnp.full((ref.shape[0], S - ref.shape[1]), value, ref.dtype)
    return jnp.concatenate([ref[...], rest], axis=1)


def place(k):
    return (k % 2) * 2 + k // 2


def sort_tiles(x_ref, i, put):
    lane = lax.broadcasted_iota(jnp.int32, (CHUNK, 128), 1)
    low = lane < 64
    even = (lane % 64) < 32
    for h in range(2):
        for c in range(J // CHUNK):
            p = [x_ref[i, pl.ds(c * 8 * CHUNK + 4 * h + g, CHUNK, stride=8), :] for g in range(4)]
            u = [None] * 4
            for a in range(2):
                turn = pltpu.roll(jnp.where(low, p[a + 2], p[a]), 64, 1)
                u[a] = jnp.where(low, p[a], turn)
                u[a + 2] = jnp.where(low, turn, p[a + 2])
            for a in range(2):
                turn = pltpu.roll(u[2 * a + 1], 32, 1)
                put(2 * a, h, c, jnp.where(even, u[2 * a], turn))
                put(2 * a + 1, h, c, jnp.where(even, turn, u[2 * a]))


def prep_kernel(
    tile_hbm, spec_hbm, x_hbm, g_ref, mhi_ref, mlo_ref, at_ref, x_ref, r_ref, tile_ref, spec_ref, sem, small_sem
):
    steps = x_hbm.shape[0]
    small = [
        pltpu.make_async_copy(tile_hbm, tile_ref, small_sem.at[0]),
        pltpu.make_async_copy(spec_hbm, spec_ref, small_sem.at[1]),
    ]
    for copy in small:
        copy.start()
    for i in range(steps):
        pltpu.make_async_copy(x_hbm.at[i], x_ref.at[i], sem.at[i]).start()
    for copy in small:
        copy.wait()
    tile = widen(tile_ref, TILES)
    here = present(tile)
    spec = widen(spec_ref, 0.0)
    spec_b = spec.astype(BF)
    spec_f = spec_b.astype(F32)
    for l in range(L8 * steps):
        block = jnp.where(here, spec_f[l : l + 1, :], 0.0).astype(BF)
        turned = (l // 4) * 4 + (l + 1) % 4
        for e, m in ((0, l), (1, turned)):
            first = (m // L8) * 512 + (m % L8) * TILES
            at_ref[e, first : first + TILES, :] = block
            at_ref[e, first + 256 : first + 256 + TILES, :] = block
    hi, lo = split(dot_t(spec_b, spec_b) * same_tile(tile))
    mhi_ref[...] = hi
    mlo_ref[...] = lo
    acc = [None] * QI
    for i in range(steps):
        pltpu.make_async_copy(x_hbm.at[i], x_ref.at[i], sem.at[i]).wait()

        def put(k, h, c, value):
            hi, lo = split(value)
            rows = slice(k * J + c * CHUNK, k * J + (c + 1) * CHUNK)
            first = i * 512 + h * 128
            r_ref[rows, first : first + 128] = hi
            r_ref[rows, first + 256 : first + 384] = lo

        sort_tiles(x_ref, i, put)
        cols = slice(i * 512, (i + 1) * 512)
        for k in range(QI):
            part = dot(r_ref[k * J : (k + 1) * J, cols], at_ref[k % 2, cols, :])
            acc[k] = part if i == 0 else acc[k] + part
    for k in range(QI):
        for n in range(2):
            g_ref[n, pl.ds(k, J, stride=QI), :] = acc[k][:, n * 128 : (n + 1) * 128]


IN_VMEM = pl.BlockSpec(memory_space=pltpu.VMEM)
IN_HBM = pl.BlockSpec(memory_space=pltpu.HBM)
CHUNK = 32


def in_hbm(x):
    return pltpu.with_memory_space_constraint(x, pltpu.HBM)


def prep(tile, spec, cube):
    steps = cube.shape[0]
    return pl.pallas_call(
        prep_kernel,
        in_specs=[IN_HBM] * 3,
        out_specs=[IN_VMEM] * 3,
        out_shape=[
            jax.ShapeDtypeStruct((2, Q, 128), F32),
            jax.ShapeDtypeStruct((S, S), BF),
            jax.ShapeDtypeStruct((S, S), BF),
        ],
        scratch_shapes=[
            pltpu.VMEM((2, 512 * steps, S), BF),
            pltpu.VMEM((steps, 2048, 128), F32),
            pltpu.VMEM((Q, 512 * steps), BF),
            pltpu.VMEM(tile.shape, jnp.int32),
            pltpu.VMEM(spec.shape, F32),
            pltpu.SemaphoreType.DMA((steps,)),
            pltpu.SemaphoreType.DMA((2,)),
        ],
        compiler_params=pltpu.CompilerParams(vmem_limit_bytes=32 << 20),
        cost_estimate=pl.CostEstimate(flops=4 * Q * 2048 * S, transcendentals=0, bytes_accessed=17 << 20),
        name="prep",
    )(in_hbm(tile), in_hbm(spec), in_hbm(cube))


def morph_kernel(m_ref, psf_hbm, g_ref, mhi_ref, mlo_ref, corr_ref, b_ref, psf_ref, sem):
    parts = Q // J
    copies = [
        pltpu.make_async_copy(psf_hbm.at[pl.ds(i * J, J)], psf_ref.at[pl.ds(i * J, J)], sem.at[i]) for i in range(parts)
    ]
    for copy in copies:
        copy.start()
    morph_b = widen(m_ref, 0.0).T
    blurred = morph_b.astype(F32)
    for i in range(parts):
        copies[i].wait()
        blurred = blurred + dot(morph_b[:, i * J : (i + 1) * J], psf_ref[i * J : (i + 1) * J, :])
    blurred = blurred.astype(BF)
    blurred_t = blurred.T
    for k in range(2):
        b_ref[k] = blurred_t[:, k * 128 : (k + 1) * 128].astype(F32)
    model = dot(blurred_t, mhi_ref[...]) + dot(blurred_t, mlo_ref[...])
    w = jnp.concatenate([g_ref[0], g_ref[1]], axis=1) - model
    corr_ref[...] = (w + dot(psf_ref[...], w.astype(BF))).astype(corr_ref.dtype)


def morph_part(morph_all, psf, g, mhi, mlo):
    return pl.pallas_call(
        morph_kernel,
        in_specs=[IN_VMEM, IN_HBM] + [IN_VMEM] * 3,
        out_shape=[jax.ShapeDtypeStruct((Q, S), BF), jax.ShapeDtypeStruct((2, Q, 128), F32)],
        scratch_shapes=[pltpu.VMEM(psf.shape, BF), pltpu.SemaphoreType.DMA((Q // J,))],
        compiler_params=pltpu.CompilerParams(vmem_limit_bytes=12 << 20),
        cost_estimate=pl.CostEstimate(flops=6 * Q * Q * S, transcendentals=0, bytes_accessed=5 << 20),
        name="morph_part",
    )(morph_all, in_hbm(psf), g, mhi, mlo)


def spec_kernel(tile_ref, spec_ref, range_ref, step_ref, b_ref, x_hbm, c_ref, base_ref, bp_ref, x_ref, r_ref, sem):
    depth = spec_ref.shape[0]
    steps = x_hbm.shape[0]
    for i in range(steps):
        pltpu.make_async_copy(x_hbm.at[i], x_ref.at[i], sem.at[i]).start()
    tile = widen(tile_ref, TILES)
    here = present(tile)[None]
    for k in range(QI):
        for n in range(2):
            rows = b_ref[n, pl.ds(k, J, stride=QI), :]
            bp_ref[n * 128 : (n + 1) * 128, place(k) * J : (place(k) + 1) * J] = rows.T.astype(BF)
    bp = bp_ref[...]
    gram = lax.dot_general(bp, bp, (((1,), (1,)), ((), ())), preferred_element_type=F32)
    bp2 = [jnp.concatenate([bp[:, e * 512 : (e + 1) * 512]] * 2, axis=1) for e in range(2)]
    hi, lo = split(gram * same_tile(tile))
    spec = widen(spec_ref, 0.0)
    spec_b = spec.astype(BF)
    lam = lax.axis_index("wave") * depth + lax.broadcasted_iota(jnp.int32, (depth, S), 0)
    ends = widen(range_ref, 0)
    inside = (lam >= ends[0:1, :]) & (lam < ends[1:2, :])
    scale = jnp.where(inside, widen(step_ref, 0.0), 0.0)
    base_ref[...] = jnp.where(inside, spec, 0.0)
    model = dot(spec_b, hi) + dot(spec_b, lo)
    for i in range(steps):
        pltpu.make_async_copy(x_hbm.at[i], x_ref.at[i], sem.at[i]).wait()

        def put(k, h, c, value):
            hi, lo = split(value)
            first = (k % 2) * 1024 + (k // 2) * J + c * CHUNK
            cols = slice(h * 128, (h + 1) * 128)
            r_ref[i, first : first + CHUNK, cols] = hi
            r_ref[i, first + 512 : first + 512 + CHUNK, cols] = lo

        sort_tiles(x_ref, i, put)
        y = [dot(bp2[e], r_ref[i, e * 1024 : (e + 1) * 1024, :]) for e in range(2)]
        for h in range(2):
            cols = slice(h * 128, (h + 1) * 128)
            y_t = (y[0][:, cols] + pltpu.roll(y[1][:, cols], 96, 1)).T.reshape(4, TILES, S)
            first = i * L8 + 4 * h
            rows = slice(first, first + 4)
            c_ref[rows, :] = scale[rows, :] * (jnp.sum(jnp.where(here, y_t, 0.0), axis=1) - model[rows, :])


def spec_part(tile, spec, ends, step, b, cube):
    return pl.pallas_call(
        spec_kernel,
        in_specs=[IN_VMEM] * 5 + [IN_HBM],
        out_specs=[IN_VMEM] * 2,
        out_shape=[jax.ShapeDtypeStruct((spec.shape[0], S), F32)] * 2,
        scratch_shapes=[
            pltpu.VMEM((S, Q), BF),
            pltpu.VMEM(cube.shape, F32),
            pltpu.VMEM((cube.shape[0], 2 * Q, 256), BF),
            pltpu.SemaphoreType.DMA(cube.shape[:1]),
        ],
        compiler_params=pltpu.CompilerParams(vmem_limit_bytes=32 << 20),
        cost_estimate=pl.CostEstimate(flops=4 * Q * 2048 * S, transcendentals=0, bytes_accessed=9 << 20),
        name="spec_part",
    )(tile, spec, ends, step, b, in_hbm(cube))


SWAP = [(0, 1), (1, 0)]


def on_device(cube, psf, spectra, morph, src_tile, wave_range, spec_step, morph_step):
    sources, depth = spectra.shape
    own = morph.shape[1]
    waves = Q // own
    morph_t = morph.T
    spec_t = spectra.T
    copies = jnp.broadcast_to(morph_t[None], (waves, own, sources)).astype(BF)
    morph_all = lax.all_to_all(copies, "wave", split_axis=0, concat_axis=0, tiled=True).reshape(Q, sources)
    groups = depth // L8
    rows = cube.reshape(groups, L8, J, 128).transpose(0, 2, 1, 3).reshape(groups, J * L8, 128)
    g, mhi, mlo = prep(src_tile, spec_t, rows)
    corr, blurred = morph_part(morph_all, psf[0, 0], g, mhi, mlo)
    parts = lax.all_to_all(corr.reshape(waves, own, S), "wave", split_axis=0, concat_axis=0, tiled=True)
    step, base = spec_part(src_tile, spec_t, wave_range.T, spec_step[None, :], blurred, rows)
    new_spectra = jnp.maximum(base + (step + lax.ppermute(step, "point", SWAP)), 0.0)[:, :sources]
    corr_morph = jnp.sum(parts.astype(F32), axis=0)
    corr_morph = (corr_morph + lax.ppermute(corr_morph, "point", SWAP))[:, :sources]
    new_morph = jnp.maximum(morph_t + morph_step[None, :] * corr_morph, 0.0)
    return (new_spectra.T, new_morph.T)


def solution(mesh):
    return jax.shard_map(
        on_device,
        mesh=mesh,
        in_specs=(
            P("point", "wave", None),
            P("point", "wave", None, None),
            P(None, "wave"),
            P(None, "wave"),
            P("point", None),
            P(),
            P(),
            P(),
        ),
        out_specs=(P(None, "wave"), P(None, "wave")),
        check_vma=False,
    )
```

```python
import jax
import jax.numpy as jnp
from jax import lax
from jax.experimental import pallas as pl
from jax.experimental.pallas import tpu as pltpu
from jax.sharding import PartitionSpec as P

BF = jnp.bfloat16
F32 = jnp.float32
S = 256
L8 = 8
TILES = 32
Q = 1024
QI = 4
J = 256


def dot(a, b):
    return jnp.dot(a, b, preferred_element_type=F32)


def dot_t(a, b):
    return lax.dot_general(a, b, (((0,), (0,)), ((), ())), preferred_element_type=F32)


def split(x):
    hi = x.astype(BF)
    return hi, (x - hi.astype(F32)).astype(BF)


def present(tile):
    return lax.broadcasted_iota(jnp.int32, (TILES, S), 0) == tile


def same_tile(tile):
    onehot = jnp.where(present(tile), 1.0, 0.0).astype(BF)
    return dot_t(onehot, onehot)


def widen(ref, value):
    rest = jnp.full((ref.shape[0], S - ref.shape[1]), value, ref.dtype)
    return jnp.concatenate([ref[...], rest], axis=1)


def place(k):
    return (k % 2) * 2 + k // 2


def sort_tiles(x_ref, i, put):
    lane = lax.broadcasted_iota(jnp.int32, (CHUNK, 128), 1)
    low = lane < 64
    even = (lane % 64) < 32
    for h in range(2):
        for c in range(J // CHUNK):
            p = [x_ref[i, pl.ds(c * 8 * CHUNK + 4 * h + g, CHUNK, stride=8), :] for g in range(4)]
            u = [None] * 4
            for a in range(2):
                turn = pltpu.roll(jnp.where(low, p[a + 2], p[a]), 64, 1)
                u[a] = jnp.where(low, p[a], turn)
                u[a + 2] = jnp.where(low, turn, p[a + 2])
            for a in range(2):
                turn = pltpu.roll(u[2 * a + 1], 32, 1)
                put(2 * a, h, c, jnp.where(even, u[2 * a], turn))
                put(2 * a + 1, h, c, jnp.where(even, turn, u[2 * a]))


def prep_kernel(
    tile_hbm, spec_hbm, x_hbm, g_ref, mhi_ref, mlo_ref, at_ref, x_ref, r_ref, tile_ref, spec_ref, sem, small_sem
):
    steps = x_hbm.shape[0]
    small = [
        pltpu.make_async_copy(tile_hbm, tile_ref, small_sem.at[0]),
        pltpu.make_async_copy(spec_hbm, spec_ref, small_sem.at[1]),
    ]
    for copy in small:
        copy.start()
    for i in range(2):
        pltpu.make_async_copy(x_hbm.at[i], x_ref.at[i], sem.at[i]).start()
    for copy in small:
        copy.wait()
    tile = widen(tile_ref, TILES)
    here = present(tile)
    spec = widen(spec_ref, 0.0)
    spec_b = spec.astype(BF)
    spec_f = spec_b.astype(F32)
    for l in range(L8 * steps):
        block = jnp.where(here, spec_f[l : l + 1, :], 0.0).astype(BF)
        turned = (l // 4) * 4 + (l + 1) % 4
        for e, m in ((0, l), (1, turned)):
            first = (m // L8) * 512 + (m % L8) * TILES
            at_ref[e, first : first + TILES, :] = block
            at_ref[e, first + 256 : first + 256 + TILES, :] = block
    hi, lo = split(dot_t(spec_b, spec_b) * same_tile(tile))
    mhi_ref[...] = hi
    mlo_ref[...] = lo
    acc = [None] * QI
    for i in range(steps):
        pltpu.make_async_copy(x_hbm.at[i], x_ref.at[i], sem.at[i]).wait()
        if i + 2 < steps:
            pltpu.make_async_copy(x_hbm.at[i + 2], x_ref.at[i + 2], sem.at[i + 2]).start()

        def put(k, h, c, value):
            hi, lo = split(value)
            rows = slice(k * J + c * CHUNK, k * J + (c + 1) * CHUNK)
            first = i * 512 + h * 128
            r_ref[rows, first : first + 128] = hi
            r_ref[rows, first + 256 : first + 384] = lo

        sort_tiles(x_ref, i, put)
        cols = slice(i * 512, (i + 1) * 512)
        for k in range(QI):
            part = dot(r_ref[k * J : (k + 1) * J, cols], at_ref[k % 2, cols, :])
            acc[k] = part if i == 0 else acc[k] + part
    for k in range(QI):
        for n in range(2):
            g_ref[n, pl.ds(k, J, stride=QI), :] = acc[k][:, n * 128 : (n + 1) * 128]


IN_VMEM = pl.BlockSpec(memory_space=pltpu.VMEM)
IN_HBM = pl.BlockSpec(memory_space=pltpu.HBM)
CHUNK = 128


def in_hbm(x):
    return pltpu.with_memory_space_constraint(x, pltpu.HBM)


def prep(tile, spec, cube):
    steps = cube.shape[0]
    return pl.pallas_call(
        prep_kernel,
        in_specs=[IN_HBM] * 3,
        out_specs=[IN_VMEM] * 3,
        out_shape=[
            jax.ShapeDtypeStruct((2, Q, 128), F32),
            jax.ShapeDtypeStruct((S, S), BF),
            jax.ShapeDtypeStruct((S, S), BF),
        ],
        scratch_shapes=[
            pltpu.VMEM((2, 512 * steps, S), BF),
            pltpu.VMEM((steps, 2048, 128), F32),
            pltpu.VMEM((Q, 512 * steps), BF),
            pltpu.VMEM(tile.shape, jnp.int32),
            pltpu.VMEM(spec.shape, F32),
            pltpu.SemaphoreType.DMA((steps,)),
            pltpu.SemaphoreType.DMA((2,)),
        ],
        compiler_params=pltpu.CompilerParams(vmem_limit_bytes=32 << 20),
        cost_estimate=pl.CostEstimate(flops=4 * Q * 2048 * S, transcendentals=0, bytes_accessed=17 << 20),
        name="prep",
    )(in_hbm(tile), in_hbm(spec), in_hbm(cube))


def morph_kernel(m_ref, psf_hbm, g_ref, mhi_ref, mlo_ref, corr_ref, b_ref, psf_ref, sem):
    parts = Q // J
    copies = [
        pltpu.make_async_copy(psf_hbm.at[pl.ds(i * J, J)], psf_ref.at[pl.ds(i * J, J)], sem.at[i]) for i in range(parts)
    ]
    for copy in copies:
        copy.start()
    morph_b = widen(m_ref, 0.0).T
    blurred = morph_b.astype(F32)
    for i in range(parts):
        copies[i].wait()
        blurred = blurred + dot(morph_b[:, i * J : (i + 1) * J], psf_ref[i * J : (i + 1) * J, :])
    blurred = blurred.astype(BF)
    blurred_t = blurred.T
    for k in range(2):
        b_ref[k] = blurred_t[:, k * 128 : (k + 1) * 128].astype(F32)
    model = dot(blurred_t, mhi_ref[...]) + dot(blurred_t, mlo_ref[...])
    w = jnp.concatenate([g_ref[0], g_ref[1]], axis=1) - model
    corr_ref[...] = (w + dot(psf_ref[...], w.astype(BF))).astype(corr_ref.dtype)


def morph_part(morph_all, psf, g, mhi, mlo):
    return pl.pallas_call(
        morph_kernel,
        in_specs=[IN_VMEM, IN_HBM] + [IN_VMEM] * 3,
        out_shape=[jax.ShapeDtypeStruct((Q, S), BF), jax.ShapeDtypeStruct((2, Q, 128), F32)],
        scratch_shapes=[pltpu.VMEM(psf.shape, BF), pltpu.SemaphoreType.DMA((Q // J,))],
        compiler_params=pltpu.CompilerParams(vmem_limit_bytes=12 << 20),
        cost_estimate=pl.CostEstimate(flops=6 * Q * Q * S, transcendentals=0, bytes_accessed=5 << 20),
        name="morph_part",
    )(morph_all, in_hbm(psf), g, mhi, mlo)


def spec_kernel(tile_ref, spec_ref, range_ref, step_ref, b_ref, x_hbm, c_ref, base_ref, bp_ref, x_ref, r_ref, sem):
    depth = spec_ref.shape[0]
    steps = x_hbm.shape[0]
    for i in range(2):
        pltpu.make_async_copy(x_hbm.at[i], x_ref.at[i], sem.at[i]).start()
    tile = widen(tile_ref, TILES)
    here = present(tile)[None]
    for k in range(QI):
        for n in range(2):
            rows = b_ref[n, pl.ds(k, J, stride=QI), :]
            bp_ref[n * 128 : (n + 1) * 128, place(k) * J : (place(k) + 1) * J] = rows.T.astype(BF)
    bp = bp_ref[...]
    gram = lax.dot_general(bp, bp, (((1,), (1,)), ((), ())), preferred_element_type=F32)
    bp2 = [jnp.concatenate([bp[:, e * 512 : (e + 1) * 512]] * 2, axis=1) for e in range(2)]
    hi, lo = split(gram * same_tile(tile))
    spec = widen(spec_ref, 0.0)
    spec_b = spec.astype(BF)
    lam = lax.axis_index("wave") * depth + lax.broadcasted_iota(jnp.int32, (depth, S), 0)
    ends = widen(range_ref, 0)
    inside = (lam >= ends[0:1, :]) & (lam < ends[1:2, :])
    scale = jnp.where(inside, widen(step_ref, 0.0), 0.0)
    base_ref[...] = jnp.where(inside, spec, 0.0)
    model = dot(spec_b, hi) + dot(spec_b, lo)
    for i in range(steps):
        pltpu.make_async_copy(x_hbm.at[i], x_ref.at[i], sem.at[i]).wait()
        if i + 2 < steps:
            pltpu.make_async_copy(x_hbm.at[i + 2], x_ref.at[i + 2], sem.at[i + 2]).start()

        def put(k, h, c, value):
            hi, lo = split(value)
            first = (k % 2) * 1024 + (k // 2) * J + c * CHUNK
            cols = slice(h * 128, (h + 1) * 128)
            r_ref[i, first : first + CHUNK, cols] = hi
            r_ref[i, first + 512 : first + 512 + CHUNK, cols] = lo

        sort_tiles(x_ref, i, put)
        y = [dot(bp2[e], r_ref[i, e * 1024 : (e + 1) * 1024, :]) for e in range(2)]
        for h in range(2):
            cols = slice(h * 128, (h + 1) * 128)
            y_t = (y[0][:, cols] + pltpu.roll(y[1][:, cols], 96, 1)).T.reshape(4, TILES, S)
            first = i * L8 + 4 * h
            rows = slice(first, first + 4)
            c_ref[rows, :] = scale[rows, :] * (jnp.sum(jnp.where(here, y_t, 0.0), axis=1) - model[rows, :])


def spec_part(tile, spec, ends, step, b, cube):
    return pl.pallas_call(
        spec_kernel,
        in_specs=[IN_VMEM] * 5 + [IN_HBM],
        out_specs=[IN_VMEM] * 2,
        out_shape=[jax.ShapeDtypeStruct((spec.shape[0], S), F32)] * 2,
        scratch_shapes=[
            pltpu.VMEM((S, Q), BF),
            pltpu.VMEM(cube.shape, F32),
            pltpu.VMEM((cube.shape[0], 2 * Q, 256), BF),
            pltpu.SemaphoreType.DMA(cube.shape[:1]),
        ],
        compiler_params=pltpu.CompilerParams(vmem_limit_bytes=32 << 20),
        cost_estimate=pl.CostEstimate(flops=4 * Q * 2048 * S, transcendentals=0, bytes_accessed=9 << 20),
        name="spec_part",
    )(tile, spec, ends, step, b, in_hbm(cube))


SWAP = [(0, 1), (1, 0)]


def on_device(cube, psf, spectra, morph, src_tile, wave_range, spec_step, morph_step):
    sources, depth = spectra.shape
    own = morph.shape[1]
    waves = Q // own
    morph_t = morph.T
    spec_t = spectra.T
    copies = jnp.broadcast_to(morph_t[None], (waves, own, sources)).astype(BF)
    morph_all = lax.all_to_all(copies, "wave", split_axis=0, concat_axis=0, tiled=True).reshape(Q, sources)
    groups = depth // L8
    rows = cube.reshape(groups, L8, J, 128).transpose(0, 2, 1, 3).reshape(groups, J * L8, 128)
    g, mhi, mlo = prep(src_tile, spec_t, rows)
    corr, blurred = morph_part(morph_all, psf[0, 0], g, mhi, mlo)
    parts = lax.all_to_all(corr.reshape(waves, own, S), "wave", split_axis=0, concat_axis=0, tiled=True)
    step, base = spec_part(src_tile, spec_t, wave_range.T, spec_step[None, :], blurred, rows)
    new_spectra = jnp.maximum(base + (step + lax.ppermute(step, "point", SWAP)), 0.0)[:, :sources]
    corr_morph = jnp.sum(parts.astype(F32), axis=0)
    corr_morph = (corr_morph + lax.ppermute(corr_morph, "point", SWAP))[:, :sources]
    new_morph = jnp.maximum(morph_t + morph_step[None, :] * corr_morph, 0.0)
    return (new_spectra.T, new_morph.T)


def solution(mesh):
    return jax.shard_map(
        on_device,
        mesh=mesh,
        in_specs=(
            P("point", "wave", None),
            P("point", "wave", None, None),
            P(None, "wave"),
            P(None, "wave"),
            P("point", None),
            P(),
            P(),
            P(),
        ),
        out_specs=(P(None, "wave"), P(None, "wave")),
        check_vma=False,
    )
```

```python
import jax
import jax.numpy as jnp
from jax import lax
from jax.experimental import pallas as pl
from jax.experimental.pallas import tpu as pltpu
from jax.sharding import PartitionSpec as P

BF = jnp.bfloat16
F32 = jnp.float32
S = 256
L8 = 8
TILES = 32
Q = 1024
QI = 4
J = 256


def dot(a, b):
    return jnp.dot(a, b, preferred_element_type=F32)


def dot_t(a, b):
    return lax.dot_general(a, b, (((0,), (0,)), ((), ())), preferred_element_type=F32)


def split(x):
    hi = x.astype(BF)
    return hi, (x - hi.astype(F32)).astype(BF)


def present(tile):
    return lax.broadcasted_iota(jnp.int32, (TILES, S), 0) == tile


def same_tile(tile):
    onehot = jnp.where(present(tile), 1.0, 0.0).astype(BF)
    return dot_t(onehot, onehot)


def widen(ref, value):
    rest = jnp.full((ref.shape[0], S - ref.shape[1]), value, ref.dtype)
    return jnp.concatenate([ref[...], rest], axis=1)


def place(k):
    return (k % 2) * 2 + k // 2


def sort_tiles(x_ref, i, put):
    lane = lax.broadcasted_iota(jnp.int32, (CHUNK, 128), 1)
    low = lane < 64
    even = (lane % 64) < 32
    for h in range(2):
        for c in range(J // CHUNK):
            p = [x_ref[i, pl.ds(c * 8 * CHUNK + 4 * h + g, CHUNK, stride=8), :] for g in range(4)]
            u = [None] * 4
            for a in range(2):
                turn = pltpu.roll(jnp.where(low, p[a + 2], p[a]), 64, 1)
                u[a] = jnp.where(low, p[a], turn)
                u[a + 2] = jnp.where(low, turn, p[a + 2])
            for a in range(2):
                turn = pltpu.roll(u[2 * a + 1], 32, 1)
                put(2 * a, h, c, jnp.where(even, u[2 * a], turn))
                put(2 * a + 1, h, c, jnp.where(even, turn, u[2 * a]))


def prep_kernel(
    tile_hbm, spec_hbm, x_hbm, g_ref, mhi_ref, mlo_ref, at_ref, x_ref, r_ref, tile_ref, spec_ref, sem, small_sem
):
    steps = x_hbm.shape[0]
    small = [
        pltpu.make_async_copy(tile_hbm, tile_ref, small_sem.at[0]),
        pltpu.make_async_copy(spec_hbm, spec_ref, small_sem.at[1]),
    ]
    for copy in small:
        copy.start()
    for i in range(AHEAD):
        pltpu.make_async_copy(x_hbm.at[i], x_ref.at[i], sem.at[i]).start()
    for copy in small:
        copy.wait()
    tile = widen(tile_ref, TILES)
    here = present(tile)
    spec = widen(spec_ref, 0.0)
    spec_b = spec.astype(BF)
    spec_f = spec_b.astype(F32)
    acc = [None] * QI

    def project(i):
        for l in range(i * L8, (i + 1) * L8):
            block = jnp.where(here, spec_f[l : l + 1, :], 0.0).astype(BF)
            turned = (l // 4) * 4 + (l + 1) % 4
            for e, m in ((0, l), (1, turned)):
                first = (m // L8) * 512 + (m % L8) * TILES
                at_ref[e, first : first + TILES, :] = block
                at_ref[e, first + 256 : first + 256 + TILES, :] = block
        cols = slice(i * 512, (i + 1) * 512)
        for k in range(QI):
            part = dot(r_ref[k * J : (k + 1) * J, cols], at_ref[k % 2, cols, :])
            acc[k] = part if i == 0 else acc[k] + part

    for i in range(steps):
        pltpu.make_async_copy(x_hbm.at[i], x_ref.at[i], sem.at[i]).wait()
        if i + AHEAD < steps:
            pltpu.make_async_copy(x_hbm.at[i + AHEAD], x_ref.at[i + AHEAD], sem.at[i + AHEAD]).start()

        def put(k, h, c, value):
            hi, lo = split(value)
            rows = slice(k * J + c * CHUNK, k * J + (c + 1) * CHUNK)
            first = i * 512 + h * 128
            r_ref[rows, first : first + 128] = hi
            r_ref[rows, first + 256 : first + 384] = lo

        if i > 0:
            project(i - 1)
        sort_tiles(x_ref, i, put)
    project(steps - 1)
    hi, lo = split(dot_t(spec_b, spec_b) * same_tile(tile))
    mhi_ref[...] = hi
    mlo_ref[...] = lo
    for k in range(QI):
        for n in range(2):
            g_ref[n, pl.ds(k, J, stride=QI), :] = acc[k][:, n * 128 : (n + 1) * 128]


IN_VMEM = pl.BlockSpec(memory_space=pltpu.VMEM)
IN_HBM = pl.BlockSpec(memory_space=pltpu.HBM)
CHUNK = 128
AHEAD = 2


def in_hbm(x):
    return pltpu.with_memory_space_constraint(x, pltpu.HBM)


def prep(tile, spec, cube):
    steps = cube.shape[0]
    return pl.pallas_call(
        prep_kernel,
        in_specs=[IN_HBM] * 3,
        out_specs=[IN_VMEM] * 3,
        out_shape=[
            jax.ShapeDtypeStruct((2, Q, 128), F32),
            jax.ShapeDtypeStruct((S, S), BF),
            jax.ShapeDtypeStruct((S, S), BF),
        ],
        scratch_shapes=[
            pltpu.VMEM((2, 512 * steps, S), BF),
            pltpu.VMEM((steps, 2048, 128), F32),
            pltpu.VMEM((Q, 512 * steps), BF),
            pltpu.VMEM(tile.shape, jnp.int32),
            pltpu.VMEM(spec.shape, F32),
            pltpu.SemaphoreType.DMA((steps,)),
            pltpu.SemaphoreType.DMA((2,)),
        ],
        compiler_params=pltpu.CompilerParams(vmem_limit_bytes=32 << 20),
        cost_estimate=pl.CostEstimate(flops=4 * Q * 2048 * S, transcendentals=0, bytes_accessed=17 << 20),
        name="prep",
    )(in_hbm(tile), in_hbm(spec), in_hbm(cube))


def morph_kernel(m_ref, psf_hbm, g_ref, mhi_ref, mlo_ref, corr_ref, b_ref, psf_ref, sem):
    parts = Q // J
    copies = [
        pltpu.make_async_copy(psf_hbm.at[pl.ds(i * J, J)], psf_ref.at[pl.ds(i * J, J)], sem.at[i]) for i in range(parts)
    ]
    for copy in copies:
        copy.start()
    morph_b = widen(m_ref, 0.0).T
    blurred = morph_b.astype(F32)
    for i in range(parts):
        copies[i].wait()
        blurred = blurred + dot(morph_b[:, i * J : (i + 1) * J], psf_ref[i * J : (i + 1) * J, :])
    blurred = blurred.astype(BF)
    blurred_t = blurred.T
    for k in range(2):
        b_ref[k] = blurred_t[:, k * 128 : (k + 1) * 128].astype(F32)
    model = dot(blurred_t, mhi_ref[...]) + dot(blurred_t, mlo_ref[...])
    w = jnp.concatenate([g_ref[0], g_ref[1]], axis=1) - model
    corr_ref[...] = (w + dot(psf_ref[...], w.astype(BF))).astype(corr_ref.dtype)


def morph_part(morph_all, psf, g, mhi, mlo):
    return pl.pallas_call(
        morph_kernel,
        in_specs=[IN_VMEM, IN_HBM] + [IN_VMEM] * 3,
        out_shape=[jax.ShapeDtypeStruct((Q, S), BF), jax.ShapeDtypeStruct((2, Q, 128), F32)],
        scratch_shapes=[pltpu.VMEM(psf.shape, BF), pltpu.SemaphoreType.DMA((Q // J,))],
        compiler_params=pltpu.CompilerParams(vmem_limit_bytes=12 << 20),
        cost_estimate=pl.CostEstimate(flops=6 * Q * Q * S, transcendentals=0, bytes_accessed=5 << 20),
        name="morph_part",
    )(morph_all, in_hbm(psf), g, mhi, mlo)


def spec_kernel(tile_ref, spec_ref, range_ref, step_ref, b_ref, x_hbm, c_ref, base_ref, bp_ref, x_ref, r_ref, sem):
    depth = spec_ref.shape[0]
    steps = x_hbm.shape[0]
    for i in range(AHEAD):
        pltpu.make_async_copy(x_hbm.at[i], x_ref.at[i], sem.at[i]).start()
    tile = widen(tile_ref, TILES)
    here = present(tile)[None]
    for k in range(QI):
        for n in range(2):
            rows = b_ref[n, pl.ds(k, J, stride=QI), :]
            bp_ref[n * 128 : (n + 1) * 128, place(k) * J : (place(k) + 1) * J] = rows.T.astype(BF)
    bp = bp_ref[...]
    gram = lax.dot_general(bp, bp, (((1,), (1,)), ((), ())), preferred_element_type=F32)
    bp2 = [jnp.concatenate([bp[:, e * 512 : (e + 1) * 512]] * 2, axis=1) for e in range(2)]
    hi, lo = split(gram * same_tile(tile))
    spec = widen(spec_ref, 0.0)
    spec_b = spec.astype(BF)
    lam = lax.axis_index("wave") * depth + lax.broadcasted_iota(jnp.int32, (depth, S), 0)
    ends = widen(range_ref, 0)
    inside = (lam >= ends[0:1, :]) & (lam < ends[1:2, :])
    scale = jnp.where(inside, widen(step_ref, 0.0), 0.0)
    base_ref[...] = jnp.where(inside, spec, 0.0)
    model = dot(spec_b, hi) + dot(spec_b, lo)
    def fold(i):
        y = [dot(bp2[e], r_ref[i, e * 1024 : (e + 1) * 1024, :]) for e in range(2)]
        for h in range(2):
            cols = slice(h * 128, (h + 1) * 128)
            y_t = (y[0][:, cols] + pltpu.roll(y[1][:, cols], 96, 1)).T.reshape(4, TILES, S)
            first = i * L8 + 4 * h
            rows = slice(first, first + 4)
            c_ref[rows, :] = scale[rows, :] * (jnp.sum(jnp.where(here, y_t, 0.0), axis=1) - model[rows, :])

    for i in range(steps):
        pltpu.make_async_copy(x_hbm.at[i], x_ref.at[i], sem.at[i]).wait()
        if i + AHEAD < steps:
            pltpu.make_async_copy(x_hbm.at[i + AHEAD], x_ref.at[i + AHEAD], sem.at[i + AHEAD]).start()

        def put(k, h, c, value):
            hi, lo = split(value)
            first = (k % 2) * 1024 + (k // 2) * J + c * CHUNK
            cols = slice(h * 128, (h + 1) * 128)
            r_ref[i, first : first + CHUNK, cols] = hi
            r_ref[i, first + 512 : first + 512 + CHUNK, cols] = lo

        if i > 0:
            fold(i - 1)
        sort_tiles(x_ref, i, put)
    fold(steps - 1)


def spec_part(tile, spec, ends, step, b, cube):
    return pl.pallas_call(
        spec_kernel,
        in_specs=[IN_VMEM] * 5 + [IN_HBM],
        out_specs=[IN_VMEM] * 2,
        out_shape=[jax.ShapeDtypeStruct((spec.shape[0], S), F32)] * 2,
        scratch_shapes=[
            pltpu.VMEM((S, Q), BF),
            pltpu.VMEM(cube.shape, F32),
            pltpu.VMEM((cube.shape[0], 2 * Q, 256), BF),
            pltpu.SemaphoreType.DMA(cube.shape[:1]),
        ],
        compiler_params=pltpu.CompilerParams(vmem_limit_bytes=32 << 20),
        cost_estimate=pl.CostEstimate(flops=4 * Q * 2048 * S, transcendentals=0, bytes_accessed=9 << 20),
        name="spec_part",
    )(tile, spec, ends, step, b, in_hbm(cube))


SWAP = [(0, 1), (1, 0)]


def on_device(cube, psf, spectra, morph, src_tile, wave_range, spec_step, morph_step):
    sources, depth = spectra.shape
    own = morph.shape[1]
    waves = Q // own
    morph_t = morph.T
    spec_t = spectra.T
    copies = jnp.broadcast_to(morph_t[None], (waves, own, sources)).astype(BF)
    morph_all = lax.all_to_all(copies, "wave", split_axis=0, concat_axis=0, tiled=True).reshape(Q, sources)
    groups = depth // L8
    rows = cube.reshape(groups, L8, J, 128).transpose(0, 2, 1, 3).reshape(groups, J * L8, 128)
    g, mhi, mlo = prep(src_tile, spec_t, rows)
    corr, blurred = morph_part(morph_all, psf[0, 0], g, mhi, mlo)
    parts = lax.all_to_all(corr.reshape(waves, own, S), "wave", split_axis=0, concat_axis=0, tiled=True)
    step, base = spec_part(src_tile, spec_t, wave_range.T, spec_step[None, :], blurred, rows)
    new_spectra = jnp.maximum(base + (step + lax.ppermute(step, "point", SWAP)), 0.0)[:, :sources]
    corr_morph = jnp.sum(parts.astype(F32), axis=0)
    corr_morph = (corr_morph + lax.ppermute(corr_morph, "point", SWAP))[:, :sources]
    new_morph = jnp.maximum(morph_t + morph_step[None, :] * corr_morph, 0.0)
    return (new_spectra.T, new_morph.T)


def solution(mesh):
    return jax.shard_map(
        on_device,
        mesh=mesh,
        in_specs=(
            P("point", "wave", None),
            P("point", "wave", None, None),
            P(None, "wave"),
            P(None, "wave"),
            P("point", None),
            P(),
            P(),
            P(),
        ),
        out_specs=(P(None, "wave"), P(None, "wave")),
        check_vma=False,
    )
```

```python
import jax
import jax.numpy as jnp
from jax import lax
from jax.experimental import pallas as pl
from jax.experimental.pallas import tpu as pltpu
from jax.sharding import PartitionSpec as P

BF = jnp.bfloat16
F32 = jnp.float32
S = 256
L8 = 8
TILES = 32
Q = 1024
QI = 4
J = 256


def dot(a, b):
    return jnp.dot(a, b, preferred_element_type=F32)


def dot_t(a, b):
    return lax.dot_general(a, b, (((0,), (0,)), ((), ())), preferred_element_type=F32)


def split(x):
    hi = x.astype(BF)
    return hi, (x - hi.astype(F32)).astype(BF)


def present(tile):
    return lax.broadcasted_iota(jnp.int32, (TILES, S), 0) == tile


def same_tile(tile):
    onehot = jnp.where(present(tile), 1.0, 0.0).astype(BF)
    return dot_t(onehot, onehot)


def widen(ref, value):
    rest = jnp.full((ref.shape[0], S - ref.shape[1]), value, ref.dtype)
    return jnp.concatenate([ref[...], rest], axis=1)


def place(k):
    return (k % 2) * 2 + k // 2


def sort_tiles(x_ref, i, put):
    lane = lax.broadcasted_iota(jnp.int32, (CHUNK, 128), 1)
    low = lane < 64
    even = (lane % 64) < 32
    for h in range(2):
        for c in range(J // CHUNK):
            p = [x_ref[i, pl.ds(c * 8 * CHUNK + 4 * h + g, CHUNK, stride=8), :] for g in range(4)]
            u = [None] * 4
            for a in range(2):
                turn = pltpu.roll(jnp.where(low, p[a + 2], p[a]), 64, 1)
                u[a] = jnp.where(low, p[a], turn)
                u[a + 2] = jnp.where(low, turn, p[a + 2])
            for a in range(2):
                turn = pltpu.roll(u[2 * a + 1], 32, 1)
                put(2 * a, h, c, jnp.where(even, u[2 * a], turn))
                put(2 * a + 1, h, c, jnp.where(even, turn, u[2 * a]))


def prep_kernel(
    tile_hbm, spec_hbm, x_hbm, psf_hbm, g_hbm, mhi_ref, mlo_ref, top_ref, g_ref, at_ref, x_ref, r_ref, tile_ref, spec_ref, sem, top_sem, g_sem, small_sem
):
    steps = x_hbm.shape[0]
    small = [
        pltpu.make_async_copy(tile_hbm, tile_ref, small_sem.at[0]),
        pltpu.make_async_copy(spec_hbm, spec_ref, small_sem.at[1]),
    ]
    for copy in small:
        copy.start()
    for i in range(AHEAD):
        pltpu.make_async_copy(x_hbm.at[i], x_ref.at[i], sem.at[i]).start()
    for copy in small:
        copy.wait()
    tile = widen(tile_ref, TILES)
    here = present(tile)
    spec = widen(spec_ref, 0.0)
    spec_b = spec.astype(BF)
    spec_f = spec_b.astype(F32)
    top = pltpu.make_async_copy(psf_hbm.at[pl.ds(0, TOP)], top_ref, top_sem)
    acc = [None] * QI

    def project(i):
        for l in range(i * L8, (i + 1) * L8):
            block = jnp.where(here, spec_f[l : l + 1, :], 0.0).astype(BF)
            turned = (l // 4) * 4 + (l + 1) % 4
            for e, m in ((0, l), (1, turned)):
                first = (m // L8) * 512 + (m % L8) * TILES
                at_ref[e, first : first + TILES, :] = block
                at_ref[e, first + 256 : first + 256 + TILES, :] = block
        cols = slice(i * 512, (i + 1) * 512)
        for k in range(QI):
            part = dot(r_ref[k * J : (k + 1) * J, cols], at_ref[k % 2, cols, :])
            acc[k] = part if i == 0 else acc[k] + part

    for i in range(steps):
        pltpu.make_async_copy(x_hbm.at[i], x_ref.at[i], sem.at[i]).wait()
        if i + AHEAD < steps:
            pltpu.make_async_copy(x_hbm.at[i + AHEAD], x_ref.at[i + AHEAD], sem.at[i + AHEAD]).start()

        if i == steps - 2:
            top.start()

        def put(k, h, c, value):
            hi, lo = split(value)
            rows = slice(k * J + c * CHUNK, k * J + (c + 1) * CHUNK)
            first = i * 512 + h * 128
            r_ref[rows, first : first + 128] = hi
            r_ref[rows, first + 256 : first + 384] = lo

        if i > 0:
            project(i - 1)
        sort_tiles(x_ref, i, put)
    project(steps - 1)
    for k in range(QI):
        for n in range(2):
            g_ref[n, pl.ds(k, J, stride=QI), :] = acc[k][:, n * 128 : (n + 1) * 128]
    store = pltpu.make_async_copy(g_ref, g_hbm, g_sem)
    store.start()
    hi, lo = split(dot_t(spec_b, spec_b) * same_tile(tile))
    mhi_ref[...] = hi
    mlo_ref[...] = lo
    top.wait()
    store.wait()


IN_VMEM = pl.BlockSpec(memory_space=pltpu.VMEM)
IN_HBM = pl.BlockSpec(memory_space=pltpu.HBM)
CHUNK = 128
AHEAD = 2
TOP = 512


def in_hbm(x):
    return pltpu.with_memory_space_constraint(x, pltpu.HBM)


def prep(tile, spec, cube, psf):
    steps = cube.shape[0]
    return pl.pallas_call(
        prep_kernel,
        in_specs=[IN_HBM] * 4,
        out_specs=[IN_HBM] + [IN_VMEM] * 3,
        out_shape=[
            pltpu.HBM((2, Q, 128), F32),
            jax.ShapeDtypeStruct((S, S), BF),
            jax.ShapeDtypeStruct((S, S), BF),
            jax.ShapeDtypeStruct((TOP, Q), BF),
        ],
        scratch_shapes=[
            pltpu.VMEM((2, Q, 128), F32),
            pltpu.VMEM((2, 512 * steps, S), BF),
            pltpu.VMEM((steps, 2048, 128), F32),
            pltpu.VMEM((Q, 512 * steps), BF),
            pltpu.VMEM(tile.shape, jnp.int32),
            pltpu.VMEM(spec.shape, F32),
            pltpu.SemaphoreType.DMA((steps,)),
            pltpu.SemaphoreType.DMA,
            pltpu.SemaphoreType.DMA,
            pltpu.SemaphoreType.DMA((2,)),
        ],
        compiler_params=pltpu.CompilerParams(vmem_limit_bytes=32 << 20),
        cost_estimate=pl.CostEstimate(flops=4 * Q * 2048 * S, transcendentals=0, bytes_accessed=17 << 20),
        name="prep",
    )(in_hbm(tile), in_hbm(spec), in_hbm(cube), in_hbm(psf))


def morph_kernel(m_ref, top_ref, psf_hbm, g_hbm, mhi_ref, mlo_ref, corr_ref, b_ref, psf_ref, g_ref, sem, g_sem):
    firsts = range(TOP, Q, J)
    copies = [
        pltpu.make_async_copy(psf_hbm.at[pl.ds(first, J)], psf_ref.at[pl.ds(first - TOP, J)], sem.at[i])
        for i, first in enumerate(firsts)
    ]
    for copy in copies:
        copy.start()
    g_load = pltpu.make_async_copy(g_hbm, g_ref, g_sem)
    g_load.start()
    morph_b = widen(m_ref, 0.0).T
    blurred = morph_b.astype(F32) + dot(morph_b[:, :TOP], top_ref[...])
    for copy, first in zip(copies, firsts):
        copy.wait()
        blurred = blurred + dot(morph_b[:, first : first + J], psf_ref[first - TOP : first - TOP + J, :])
    blurred = blurred.astype(BF)
    blurred_t = blurred.T
    for k in range(2):
        b_ref[k] = blurred_t[:, k * 128 : (k + 1) * 128].astype(F32)
    model = dot(blurred_t, mhi_ref[...]) + dot(blurred_t, mlo_ref[...])
    g_load.wait()
    w = jnp.concatenate([g_ref[0], g_ref[1]], axis=1) - model
    w_b = w.astype(BF)
    corr_ref[:TOP, :] = (w[:TOP] + dot(top_ref[...], w_b)).astype(BF)
    corr_ref[TOP:, :] = (w[TOP:] + dot(psf_ref[...], w_b)).astype(BF)


def morph_part(morph_all, top, psf, g, mhi, mlo):
    return pl.pallas_call(
        morph_kernel,
        in_specs=[IN_VMEM] * 2 + [IN_HBM] * 2 + [IN_VMEM] * 2,
        out_shape=[jax.ShapeDtypeStruct((Q, S), BF), jax.ShapeDtypeStruct((2, Q, 128), F32)],
        scratch_shapes=[
            pltpu.VMEM((Q - TOP, Q), BF),
            pltpu.VMEM(g.shape, F32),
            pltpu.SemaphoreType.DMA(((Q - TOP) // J,)),
            pltpu.SemaphoreType.DMA,
        ],
        compiler_params=pltpu.CompilerParams(vmem_limit_bytes=12 << 20),
        cost_estimate=pl.CostEstimate(flops=6 * Q * Q * S, transcendentals=0, bytes_accessed=5 << 20),
        name="morph_part",
    )(morph_all, top, in_hbm(psf), in_hbm(g), mhi, mlo)


def spec_kernel(tile_ref, spec_ref, range_ref, step_ref, b_ref, x_hbm, c_ref, base_ref, bp_ref, x_ref, r_ref, sem):
    depth = spec_ref.shape[0]
    steps = x_hbm.shape[0]
    for i in range(AHEAD):
        pltpu.make_async_copy(x_hbm.at[i], x_ref.at[i], sem.at[i]).start()
    tile = widen(tile_ref, TILES)
    here = present(tile)[None]
    for k in range(QI):
        for n in range(2):
            rows = b_ref[n, pl.ds(k, J, stride=QI), :]
            bp_ref[n * 128 : (n + 1) * 128, place(k) * J : (place(k) + 1) * J] = rows.T.astype(BF)
    bp = bp_ref[...]
    gram = lax.dot_general(bp, bp, (((1,), (1,)), ((), ())), preferred_element_type=F32)
    bp2 = [jnp.concatenate([bp[:, e * 512 : (e + 1) * 512]] * 2, axis=1) for e in range(2)]
    hi, lo = split(gram * same_tile(tile))
    spec = widen(spec_ref, 0.0)
    spec_b = spec.astype(BF)
    lam = lax.axis_index("wave") * depth + lax.broadcasted_iota(jnp.int32, (depth, S), 0)
    ends = widen(range_ref, 0)
    inside = (lam >= ends[0:1, :]) & (lam < ends[1:2, :])
    scale = jnp.where(inside, widen(step_ref, 0.0), 0.0)
    base_ref[...] = jnp.where(inside, spec, 0.0)
    model = dot(spec_b, hi) + dot(spec_b, lo)
    def fold(i):
        y = [dot(bp2[e], r_ref[i, e * 1024 : (e + 1) * 1024, :]) for e in range(2)]
        for h in range(2):
            cols = slice(h * 128, (h + 1) * 128)
            y_t = (y[0][:, cols] + pltpu.roll(y[1][:, cols], 96, 1)).T.reshape(4, TILES, S)
            first = i * L8 + 4 * h
            rows = slice(first, first + 4)
            c_ref[rows, :] = scale[rows, :] * (jnp.sum(jnp.where(here, y_t, 0.0), axis=1) - model[rows, :])

    for i in range(steps):
        pltpu.make_async_copy(x_hbm.at[i], x_ref.at[i], sem.at[i]).wait()
        if i + AHEAD < steps:
            pltpu.make_async_copy(x_hbm.at[i + AHEAD], x_ref.at[i + AHEAD], sem.at[i + AHEAD]).start()

        def put(k, h, c, value):
            hi, lo = split(value)
            first = (k % 2) * 1024 + (k // 2) * J + c * CHUNK
            cols = slice(h * 128, (h + 1) * 128)
            r_ref[i, first : first + CHUNK, cols] = hi
            r_ref[i, first + 512 : first + 512 + CHUNK, cols] = lo

        if i > 0:
            fold(i - 1)
        sort_tiles(x_ref, i, put)
    fold(steps - 1)


def spec_part(tile, spec, ends, step, b, cube):
    return pl.pallas_call(
        spec_kernel,
        in_specs=[IN_VMEM] * 5 + [IN_HBM],
        out_specs=[IN_VMEM] * 2,
        out_shape=[jax.ShapeDtypeStruct((spec.shape[0], S), F32)] * 2,
        scratch_shapes=[
            pltpu.VMEM((S, Q), BF),
            pltpu.VMEM(cube.shape, F32),
            pltpu.VMEM((cube.shape[0], 2 * Q, 256), BF),
            pltpu.SemaphoreType.DMA(cube.shape[:1]),
        ],
        compiler_params=pltpu.CompilerParams(vmem_limit_bytes=32 << 20),
        cost_estimate=pl.CostEstimate(flops=4 * Q * 2048 * S, transcendentals=0, bytes_accessed=9 << 20),
        name="spec_part",
    )(tile, spec, ends, step, b, in_hbm(cube))


SWAP = [(0, 1), (1, 0)]


def on_device(cube, psf, spectra, morph, src_tile, wave_range, spec_step, morph_step):
    sources, depth = spectra.shape
    own = morph.shape[1]
    waves = Q // own
    morph_t = morph.T
    spec_t = spectra.T
    copies = jnp.broadcast_to(morph_t[None], (waves, own, sources)).astype(BF)
    morph_all = lax.all_to_all(copies, "wave", split_axis=0, concat_axis=0, tiled=True).reshape(Q, sources)
    groups = depth // L8
    rows = cube.reshape(groups, L8, J, 128).transpose(0, 2, 1, 3).reshape(groups, J * L8, 128)
    g, mhi, mlo, top = prep(src_tile, spec_t, rows, psf[0, 0])
    corr, blurred = morph_part(morph_all, top, psf[0, 0], g, mhi, mlo)
    parts = lax.all_to_all(corr.reshape(waves, own, S), "wave", split_axis=0, concat_axis=0, tiled=True)
    step, base = spec_part(src_tile, spec_t, wave_range.T, spec_step[None, :], blurred, rows)
    new_spectra = jnp.maximum(base + (step + lax.ppermute(step, "point", SWAP)), 0.0)[:, :sources]
    corr_morph = jnp.sum(parts.astype(F32), axis=0)
    corr_morph = (corr_morph + lax.ppermute(corr_morph, "point", SWAP))[:, :sources]
    new_morph = jnp.maximum(morph_t + morph_step[None, :] * corr_morph, 0.0)
    return (new_spectra.T, new_morph.T)


def solution(mesh):
    return jax.shard_map(
        on_device,
        mesh=mesh,
        in_specs=(
            P("point", "wave", None),
            P("point", "wave", None, None),
            P(None, "wave"),
            P(None, "wave"),
            P("point", None),
            P(),
            P(),
            P(),
        ),
        out_specs=(P(None, "wave"), P(None, "wave")),
        check_vma=False,
    )
```
